32 devices in a mesh: grp: 4 (over x, core), seq: 8 (over z, y).
Axes of the slice: x: 2, y: 2, z: 4, core: 2. Of those that a mesh axis runs over, the one named last changes fastest.
Arguments:
- queries: bfloat16 [12288, 4096], P(('grp', 'seq')), may hold values from -6 to 6
- keys: bfloat16 [12288, 4096], P(('grp', 'seq')), may hold values from -6 to 6
- values: bfloat16 [12288, 4096], P(('grp', 'seq')), may hold values from -6 to 6
- gain: bfloat16 [4096], replicated, may hold values from 0.5 to 1.5
Outputs:
- attended: bfloat16 [12288, 4096], P(('grp', 'seq'))
The draws below stay inside these ranges and needn't reach their ends.
All inputs are finite; a program needn't handle non-finite values.
Results may differ from the reference program's by a relative error of at most 0.0053.
Values sent between devices are 32-bit elements; how exact they have to be, the bound alone decides.
No kernel may reach another device: no remote copies, remote signals or barrier semaphores. Data moves between devices by JAX's collectives and lax.ppermute only.
A program may use at most 256 MiB of HBM per device.

```python
import jax
import jax.numpy as jnp
from jax import lax

HEADS = 32
HEAD_DIM = 128
D = 4096
TOK_DEV = 384
TOKENS = 12288


def shard_levels(stream_key, dims, cuts, low, top_value):
    loudness, own = 1.0, jax.random.fold_in(stream_key, 6)
    for dim, shards_of in cuts:
        draws = jnp.exp(jax.random.uniform(jax.random.fold_in(own, dim), (shards_of,), jnp.float32, low / len(cuts), top_value / len(cuts)))
        loudness = loudness * jnp.repeat(draws, dims[dim] // shards_of).reshape([-1 if axis == dim else 1 for axis in range(len(dims))])
    return loudness


def normal_values(own_key, dims, scale, reach, cuts=(), kind=jnp.bfloat16):
    factor_of = shard_levels(own_key, dims, cuts, -0.22, 0.18) if cuts else 1.0
    values = jax.random.normal(own_key, dims, jnp.float32) * scale * factor_of
    return jnp.minimum(jnp.maximum(values, -reach), reach).astype(kind)


def setup_inputs(seed: int = 0) -> dict:
    splits = jax.random.split(jax.random.key(seed), 5)
    queries = normal_values(splits[0], (TOKENS, D), 1.0, 6.0, ((0, 32),))
    keys = normal_values(splits[1], (TOKENS, D), 1.0, 6.0, ((0, 32),))
    values = normal_values(splits[2], (TOKENS, D), 1.0, 6.0, ((0, 32),))
    gain = jnp.clip(1.0 + 0.1 * jax.random.normal(splits[3], (D,), jnp.float32), 0.5, 1.5).astype(jnp.bfloat16)
    return {"queries": queries, "keys": keys, "values": values, "gain": gain}


def reference(queries, keys, values, gain):
    shards = TOKENS // TOK_DEV
    fq = jax.nn.silu(queries.astype(jnp.float32)).astype(jnp.bfloat16)
    fk = jax.nn.silu(keys.astype(jnp.float32)).astype(jnp.bfloat16)
    fq = fq.reshape(shards, TOK_DEV, HEADS, HEAD_DIM)
    fk = fk.reshape(shards, TOK_DEV, HEADS, HEAD_DIM)
    vals = values.reshape(shards, TOK_DEV, HEADS, HEAD_DIM)
    gains = gain.astype(jnp.float32).reshape(HEADS, HEAD_DIM)
    rows = jnp.arange(TOK_DEV, dtype=jnp.int32)
    causal = rows[:, None] >= rows[None, :]

    def one_block(carry, block):
        bq, bk, bv = block
        bq32 = bq.astype(jnp.float32)
        bk32 = bk.astype(jnp.float32)
        bv32 = bv.astype(jnp.float32)
        scores = jnp.einsum('thd,shd->hts', bq32, bk32)
        scores = jnp.where(causal[None], scores, 0.0).astype(jnp.bfloat16)
        intra = jnp.einsum('hts,she->the', scores.astype(jnp.float32), bv32)
        state_b16 = carry.astype(jnp.bfloat16)
        inter = jnp.einsum('thd,hde->the', bq32, state_b16.astype(jnp.float32))
        mixed = intra + inter
        meansq = lax.optimization_barrier(jnp.mean(mixed * mixed, axis=-1, keepdims=True))
        normed = mixed * lax.rsqrt(meansq + 1e-06) * gains[None]
        local = jnp.einsum('thd,the->hde', bk32, bv32)
        return (carry + local, normed.astype(jnp.bfloat16))
    start = jnp.zeros((HEADS, HEAD_DIM, HEAD_DIM), jnp.float32)
    final, outs = lax.scan(one_block, start, (fq, fk, vals))
    return outs.reshape(TOKENS, D)
```

```python
import functools

import jax
import jax.numpy as jnp
from jax import lax
from jax.experimental import pallas as pl
from jax.experimental.pallas import tpu as pltpu
from jax.sharding import PartitionSpec as P

HEAD_DIM = 128
QUAD = 4
AXES = ("grp", "seq")
CHUNKS = (16, 16)


def silu16(u):
    u = u.astype(jnp.float32)
    return (u / (1.0 + jnp.exp(-u))).astype(jnp.bfloat16)


def kv_body(me_ref, k_ref, v_ref, *outs):
    d = pl.program_id(0)
    for slot, out in enumerate(outs):

        @pl.when(d == slot)
        def _(out=out):
            for h in range(out.shape[0]):
                cols = slice(h * HEAD_DIM, (h + 1) * HEAD_DIM)
                out[h] = lax.dot_general(
                    silu16(k_ref[:, cols]),
                    v_ref[:, cols],
                    (((0,), (0,)), ((), ())),
                    preferred_element_type=jnp.float32,
                )


def kv_states(me, keys, values, start, heads):
    rows = keys.shape[0]
    hs = heads // QUAD
    width = hs * HEAD_DIM
    spec = pl.BlockSpec((rows, width), lambda d, me_ref: (0, start // hs + (d ^ me_ref[0])))
    out_spec = pl.BlockSpec((hs, HEAD_DIM, HEAD_DIM), lambda d, me_ref: (0, 0, 0))
    return pl.pallas_call(
        kv_body,
        out_shape=[jax.ShapeDtypeStruct((hs, HEAD_DIM, HEAD_DIM), jnp.float32)] * QUAD,
        grid_spec=pltpu.PrefetchScalarGridSpec(
            num_scalar_prefetch=1,
            grid=(QUAD,),
            in_specs=[spec, spec],
            out_specs=[out_spec] * QUAD,
        ),
        cost_estimate=pl.CostEstimate(
            flops=2 * rows * heads * HEAD_DIM * HEAD_DIM,
            bytes_accessed=4 * rows * heads * HEAD_DIM + 4 * heads * HEAD_DIM * HEAD_DIM,
            transcendentals=rows * heads * HEAD_DIM,
        ),
        name="kv",
    )(me, keys, values)


def intra_body(q_ref, k_ref, v_ref, fq_ref, intra_ref):
    rows, width = q_ref.shape
    tile = HEAD_DIM
    at = lax.broadcasted_iota(jnp.int32, (tile, tile), 0)
    to = lax.broadcasted_iota(jnp.int32, (tile, tile), 1)
    causal = at >= to
    for h in range(width // HEAD_DIM):
        cols = slice(h * HEAD_DIM, (h + 1) * HEAD_DIM)
        fq = silu16(q_ref[:, cols])
        fk = silu16(k_ref[:, cols])
        vals = v_ref[:, cols]
        fq_ref[:, cols] = fq
        for t in range(rows // tile):
            span = (t + 1) * tile
            scores = lax.dot_general(
                fq[t * tile : span],
                fk[:span],
                (((1,), (1,)), ((), ())),
                preferred_element_type=jnp.float32,
            )
            last = jnp.where(causal, scores[:, t * tile :], 0.0)
            if t:
                scores = jnp.concatenate([scores[:, : t * tile], last], axis=1)
            else:
                scores = last
            intra_ref[t * tile : span, cols] = jnp.dot(
                scores.astype(jnp.bfloat16), vals[:span], preferred_element_type=jnp.float32
            )


def intra_part(queries, keys, values, start, heads):
    rows = keys.shape[0]
    hs = heads // QUAD
    width = hs * HEAD_DIM
    spec = pl.BlockSpec((rows, width), lambda i: (0, start // hs + i))
    out_spec = pl.BlockSpec((rows, width), lambda i: (0, i))
    return pl.pallas_call(
        intra_body,
        out_shape=[
            jax.ShapeDtypeStruct((rows, heads * HEAD_DIM), jnp.bfloat16),
            jax.ShapeDtypeStruct((rows, heads * HEAD_DIM), jnp.float32),
        ],
        grid=(QUAD,),
        in_specs=[spec] * 3,
        out_specs=[out_spec] * 2,
        cost_estimate=pl.CostEstimate(
            flops=4 * rows * rows * heads * HEAD_DIM,
            bytes_accessed=12 * rows * heads * HEAD_DIM,
            transcendentals=2 * rows * heads * HEAD_DIM,
        ),
        name="intra",
    )(queries, keys, values)


def final_body(me_ref, fq_ref, intra_ref, gain_ref, *refs):
    slots, state, out_ref = refs[:QUAD], refs[-1], refs[-2]
    d = pl.program_id(0)
    for slot, ref in enumerate(slots):

        @pl.when(d == slot)
        def _(ref=ref):
            state[...] = ref[...].astype(jnp.bfloat16)

    for h in range(state.shape[0]):
        cols = slice(h * HEAD_DIM, (h + 1) * HEAD_DIM)
        mixed = intra_ref[:, cols] + jnp.dot(
            fq_ref[:, cols], state[h], preferred_element_type=jnp.float32
        )
        meansq = jnp.mean(mixed * mixed, axis=-1, keepdims=True)
        gains = gain_ref[:, cols].astype(jnp.float32)
        out_ref[:, cols] = (mixed * lax.rsqrt(meansq + 1e-06) * gains).astype(jnp.bfloat16)


def finish(me, fq, intra, gain, slots, start, heads, whole):
    rows = fq.shape[0]
    hs = heads // QUAD
    width = hs * HEAD_DIM
    part = lambda d, me_ref: (0, d ^ me_ref[0])
    full = lambda d, me_ref: (0, start // hs + (d ^ me_ref[0]))
    slot_spec = pl.BlockSpec((hs, HEAD_DIM, HEAD_DIM), lambda d, me_ref: (0, 0, 0))
    in_specs = [
        pl.BlockSpec((rows, width), part),
        pl.BlockSpec((rows, width), part),
        pl.BlockSpec((1, width), full),
    ] + [slot_spec] * QUAD
    operands = [me, fq, intra, gain, *slots]
    aliases = {}
    if whole is not None:
        aliases = {len(operands): 0}
        operands.append(whole)
        in_specs.append(pl.BlockSpec(memory_space=pl.ANY))
    return pl.pallas_call(
        final_body,
        out_shape=jax.ShapeDtypeStruct((rows, gain.shape[1]), jnp.bfloat16),
        grid_spec=pltpu.PrefetchScalarGridSpec(
            num_scalar_prefetch=1,
            grid=(QUAD,),
            in_specs=in_specs,
            out_specs=pl.BlockSpec((rows, width), full),
            scratch_shapes=[pltpu.VMEM((hs, HEAD_DIM, HEAD_DIM), jnp.bfloat16)],
        ),
        input_output_aliases=aliases,
        cost_estimate=pl.CostEstimate(
            flops=2 * rows * heads * HEAD_DIM * HEAD_DIM,
            bytes_accessed=8 * rows * heads * HEAD_DIM,
            transcendentals=rows * heads,
        ),
        name="finish",
    )(*operands)


def swap(value, bit, count):
    return lax.ppermute(value, AXES, [(i, i ^ bit) for i in range(count)])


def scan_slots(slots, index, count):
    got = [slots[0]] + [swap(slots[d], d, count) for d in range(1, QUAD)]
    total = got[0] + got[1] + got[2] + got[3]
    carried = None
    bit = QUAD
    while bit < count:
        other = swap(total, bit, count)
        after = (index & bit) != 0
        term = jnp.where(after, other, 0.0)
        carried = term if carried is None else carried + term
        total = total + other
        bit *= 2
    sends = []
    for d in range(QUAD):
        acc = carried
        for e in range(QUAD):
            if e != d:
                top = 2 if (d ^ e) & 2 else 1
                later = ((index ^ d) & top) != 0
                acc = acc + jnp.where(later, got[e], 0.0)
        sends.append(acc)
    return [sends[0]] + [swap(sends[d], d, count) for d in range(1, QUAD)]


def shards(queries, keys, values, gain):
    count = lax.axis_size(AXES)
    index = lax.axis_index(AXES)
    assert count & (count - 1) == 0 and lax.axis_size("seq") % QUAD == 0
    me = jnp.reshape(index & (QUAD - 1), (1,)).astype(jnp.int32)
    gains = gain.reshape(1, -1)
    parts, start = [], 0
    for heads in CHUNKS:
        slots = kv_states(me, keys, values, start, heads)
        parts.append((start, heads, scan_slots(slots, index, count)))
        start += heads
    assert start * HEAD_DIM == keys.shape[1]
    out = None
    for start, heads, slots in parts:
        fq, intra = intra_part(queries, keys, values, start, heads)
        out = finish(me, fq, intra, gains, slots, start, heads, out)
    return out


def solution(mesh):
    split = P(AXES, None)
    return jax.shard_map(
        shards, mesh=mesh, in_specs=(split, split, split, P()), out_specs=split, check_vma=False
    )
```
